32 devices in a mesh: row: 2 (over y), col: 16 (over z, x, core).
Axes of the slice: x: 2, y: 2, z: 4, core: 2. Of those that a mesh axis runs over, the one named last changes fastest.
Arguments:
- side_a: float32 [16, 8192], P('row', 'col'), may hold values from -6 to 6
- side_b: float32 [512, 8192], P('col', 'row'), may hold values from -6 to 6
- pair_grad: float32 [16, 512, 128], P('row', 'col'), may hold values from -6 to 6
- out_weight: float32 [1024, 128], replicated, may hold values from -0.1875 to 0.1875
Outputs:
- grad_a: float32 [16, 8192], P('row', 'col')
- grad_b: float32 [512, 8192], P('col', 'row')
- grad_weight: float32 [1024, 128], replicated
- grad_bias: float32 [128], replicated
The draws below stay inside these ranges and needn't reach their ends.
All inputs are finite; a program needn't handle non-finite values.
Results may differ from the reference program's by a relative error of at most 0.00013.
Values sent between devices are 32-bit elements; how exact they have to be, the bound alone decides.
No kernel may reach another device: no remote copies, remote signals or barrier semaphores. Data moves between devices by JAX's collectives and lax.ppermute only.
A program may use at most 64 MiB of HBM per device.

```python
import math
import jax
import jax.numpy as jnp
from jax import lax

S = 256
C = 32
P_SIZE = 128
LI = 16
LJ = 512


def steps_of(stream_key, dims, cuts, smallest, top_value):
    loudness = 1.0
    for axis_at, blocks in cuts:
        draws = jax.random.uniform(jax.random.fold_in(jax.random.fold_in(stream_key, 6), axis_at), (blocks,), jnp.float32, smallest / len(cuts), top_value / len(cuts))
        loudness = loudness * jnp.repeat(jnp.exp(draws), dims[axis_at] // blocks).reshape((-1,) + (1,) * (len(dims) - 1 - axis_at))
    return loudness


def normal_values(rng, dims, width, bound, shards=(), dtype=jnp.bfloat16):
    gain = steps_of(rng, dims, shards, -0.22, 0.18) if shards else 1.0
    result = jax.random.normal(rng, dims, jnp.float32) * width * gain
    return jnp.minimum(jnp.maximum(result, -bound), bound).astype(dtype)


def setup_inputs(seed: int = 0) -> dict:
    key_list = jax.random.split(jax.random.key(seed), 5)
    side_a = normal_values(key_list[0], (LI, S * C), 1.0, 6.0, ((0, 2), (1, 16)), jnp.float32)
    side_b = normal_values(key_list[1], (LJ, S * C), 1.0, 6.0, ((0, 16), (1, 2)), jnp.float32)
    pair_grad = normal_values(key_list[2], (LI, LJ, P_SIZE), 1.0, 6.0, ((0, 2), (1, 16)), jnp.float32)
    out_weight = normal_values(key_list[3], (C * C, P_SIZE), (C * C) ** -0.5, 0.1875, (), jnp.float32)
    return {"side_a": side_a, "side_b": side_b, "pair_grad": pair_grad, "out_weight": out_weight}


def tile_terms(left_piece, right_flat, pair_piece, out_weight):
    high = lax.Precision.HIGHEST
    rows = left_piece.shape[0]
    cols = right_flat.shape[1] // C
    left_flat = jnp.transpose(left_piece, (0, 2, 1)).reshape(rows * C, S)
    flat_pair = pair_piece.reshape(rows * cols, P_SIZE)
    grad_outer = jnp.dot(flat_pair, out_weight.T, precision=high)
    grad_tile = jnp.transpose(grad_outer.reshape(rows, cols, C, C), (0, 2, 1, 3)).reshape(rows * C, cols * C)
    left_grad = jnp.dot(grad_tile, right_flat.T, precision=high) / S
    left_grad = jnp.transpose(left_grad.reshape(rows, C, S), (0, 2, 1))
    right_grad = jnp.dot(left_flat.T, grad_tile, precision=high) / S
    outer = jnp.dot(left_flat, right_flat, precision=high) / S
    outer = jnp.transpose(outer.reshape(rows, C, cols, C), (0, 2, 1, 3)).reshape(rows * cols, C * C)
    weight_part = jnp.dot(outer.T, flat_pair, precision=high)
    return left_grad, right_grad, weight_part


def reference(side_a, side_b, pair_grad, out_weight):
    left = side_a.reshape(LI, S, C)
    right = side_b.reshape(LJ, S, C)
    right_flat = jnp.transpose(right, (1, 0, 2)).reshape(S, LJ * C)
    block = math.gcd(LI, 8)
    left_blocks = left.reshape(LI // block, block, S, C)
    pair_blocks = pair_grad.reshape(LI // block, block, LJ, P_SIZE)

    def step(carry, pieces):
        right_total, weight_total = carry
        left_piece, pair_piece = pieces
        left_grad, right_part, weight_part = tile_terms(left_piece, right_flat, pair_piece, out_weight)
        return (right_total + right_part, weight_total + weight_part), left_grad

    start = (jnp.zeros((S, LJ * C), jnp.float32), jnp.zeros((C * C, P_SIZE), jnp.float32))
    (right_total, weight_total), left_grads = lax.scan(step, start, (left_blocks, pair_blocks))
    grad_a = left_grads.reshape(LI, S * C)
    grad_b = jnp.transpose(right_total.reshape(S, LJ, C), (1, 0, 2)).reshape(LJ, S * C)
    grad_bias = jnp.sum(pair_grad, axis=(0, 1))
    return grad_a, grad_b, weight_total, grad_bias
```

```python
import math

import jax
import jax.numpy as jnp
from jax import lax
from jax.experimental import pallas as pl
from jax.experimental.pallas import tpu as pltpu
from jax.sharding import PartitionSpec as P

LANES = 128
NT = (((1,), (1,)), ((), ()))
NN = (((1,), (0,)), ((), ()))


def split(x):
    hi = x.astype(jnp.bfloat16)
    lo = (x - hi.astype(jnp.float32)).astype(jnp.bfloat16)
    return hi, lo


def dot3(a, b, dims):
    def one(u, v):
        return lax.dot_general(u, v, dims, preferred_element_type=jnp.float32)

    return one(a[0], b[0]) + (one(a[0], b[1]) + one(a[1], b[0]))


def swap_blocks(parts):
    n = len(parts)
    width = LANES // n
    block = lax.broadcasted_iota(jnp.int32, parts[0].shape, 1) // width
    step = 1
    while step < n:
        low = (block & step) == 0
        done = list(parts)
        for t in range(n):
            if t & step == 0:
                p, r = parts[t], parts[t + step]
                done[t] = jnp.where(low, p, pltpu.roll(r, step * width, 1))
                done[t + step] = jnp.where(low, pltpu.roll(p, LANES - step * width, 1), r)
        parts = done
        step *= 2
    return parts


def place(m, order):
    p = 0
    for k, bit in enumerate(order):
        p = p | (((m >> bit) & 1) << k)
    return p


class Dims:
    def __init__(self, mesh, side_a, side_b, pair_grad, out_weight):
        self.R, self.Q = mesh.shape["row"], mesh.shape["col"]
        self.rows, self.cols, self.K = pair_grad.shape
        self.CE = out_weight.shape[0]
        self.C = math.isqrt(self.CE)
        self.S = side_a.shape[1] * self.Q // self.C
        self.n = LANES // self.C
        self.G = self.C // self.n
        self.slab = self.S // self.R
        self.g = self.slab // self.n
        self.blk = side_a.shape[1]
        self.gb = self.blk // LANES
        self.per = self.Q // self.R
        self.IC = self.rows * self.C
        self.JE = self.cols * self.C


def first_kernel(d, pg_ref, w_ref, b_ref, gh_ref, gl_ref, bh_ref, bl_ref, t_ref, tb_ref):
    pg = split(pg_ref[...].reshape(d.rows * d.cols, d.K))
    pairs = d.rows * d.cols
    two = 2 if d.G % 2 == 0 else 1
    for u in range(0, d.G, two):
        w = jnp.concatenate(
            [w_ref[pl.ds((p4 * d.G + v) * d.C, d.C), :] for v in range(u, u + two) for p4 in range(d.n)], axis=0
        )
        out = dot3(pg, split(w), NT)
        for v in range(two):
            t_ref[pl.ds((u + v) * pairs, pairs), :] = out[:, v * LANES:(v + 1) * LANES]

    def body(i, carry):
        for quad in range(d.cols // d.n):
            parts = [t_ref[pl.ds(i * d.cols + quad * d.n + t, d.G, stride=pairs), :] for t in range(d.n)]
            hi, lo = split(jnp.concatenate(swap_blocks(parts), axis=0))
            at = pl.multiple_of(i * d.C, d.C)
            gh_ref[pl.ds(at, d.C), quad * LANES:(quad + 1) * LANES] = hi
            gl_ref[pl.ds(at, d.C), quad * LANES:(quad + 1) * LANES] = lo
        return carry

    lax.fori_loop(0, d.rows, body, 0)
    to_seq(d, b_ref, bh_ref, bl_ref, 0, tb_ref)


def to_seq(d, b_ref, bh_ref, bl_ref, at, tb_ref):
    for v in range(d.g):
        tb_ref[pl.ds(v * d.cols, d.cols), :] = b_ref[:, v * LANES:(v + 1) * LANES]
    for quad in range(d.cols // d.n):
        parts = [tb_ref[pl.ds(quad * d.n + t, d.g, stride=d.cols), :] for t in range(d.n)]
        hi, lo = split(jnp.concatenate(swap_blocks(parts), axis=0))
        bh_ref[at:at + d.slab, quad * LANES:(quad + 1) * LANES] = hi
        bl_ref[at:at + d.slab, quad * LANES:(quad + 1) * LANES] = lo


def second_kernel(d, order, blocks, pg_ref, a_ref, bx_ref, bh_ref, bl_ref, w_ref, ah_ref, al_ref, xh_ref, xl_ref,
                  t_ref, tb_ref, ta_ref, o_ref):
    r, q = lax.axis_index("row"), lax.axis_index("col")
    pairs = d.rows * d.cols
    xh_ref[0:d.slab, :] = bh_ref[...]
    xl_ref[0:d.slab, :] = bl_ref[...]
    for m in range(1, d.R):
        to_seq(d, bx_ref.at[m - 1], xh_ref, xl_ref, m * d.slab, tb_ref)
    for m in range(d.R):
        for k in range(d.per):
            src = place(((r ^ m) * d.per + k) ^ q, order)
            for v in range(d.gb):
                ta_ref[pl.ds((k * d.gb + v) * d.rows, d.rows), :] = a_ref[src, :, v * LANES:(v + 1) * LANES]
        for quad in range(d.rows // d.n):
            parts = [ta_ref[pl.ds(quad * d.n + t, d.g, stride=d.rows), :] for t in range(d.n)]
            o_ref[m * d.slab:(m + 1) * d.slab, quad * LANES:(quad + 1) * LANES] = jnp.concatenate(
                swap_blocks(parts), axis=0) * (1.0 / d.S)
    a = o_ref[0:d.S, 0:d.IC]
    hi, lo = split(a)
    ah_ref[...] = hi
    al_ref[...] = lo
    o_ref[0:d.IC, :] = dot3(split(a.T), (xh_ref[...], xl_ref[...]), NN)

    def body(i, carry):
        for quad in range(d.cols // d.n):
            parts = [o_ref[pl.ds(pl.multiple_of(i * d.C + p4 * d.G, d.G), d.G), quad * LANES:(quad + 1) * LANES]
                     for p4 in range(d.n)]
            for t, x in enumerate(swap_blocks(parts)):
                t_ref[pl.ds(i * d.cols + quad * d.n + t, d.G, stride=pairs), :] = x
        return carry

    lax.fori_loop(0, d.rows, body, 0)
    flat = pg_ref[...].reshape(pairs, d.K)
    turned = split(flat.T)
    beta = blocks.mine()
    per = d.CE // blocks.count
    for u in range(d.G):
        part = dot3(turned, split(t_ref[pl.ds(u * pairs, pairs), :]), NN).T
        for p4 in range(d.n):
            row = (p4 * d.G + u) * d.C
            w_ref[(row // per) ^ beta, pl.ds(row % per, d.C), :] = part[p4 * d.C:(p4 + 1) * d.C]
    bias = jnp.broadcast_to(jnp.sum(flat, axis=0, keepdims=True), (8, d.K))
    for t in range(blocks.count):
        w_ref[t, pl.ds(per, 8), :] = bias


def third_kernel(d, order, gh_ref, gl_ref, ah_ref, al_ref, xh_ref, xl_ref, gb_ref, ga_ref, tb_ref, ta_ref, o_ref):
    r, q = lax.axis_index("row"), lax.axis_index("col")
    gt = gh_ref[...], gl_ref[...]
    for m in range(d.R):
        at = slice(m * d.slab, (m + 1) * d.slab)
        o_ref[0:d.slab, :] = dot3((ah_ref[at, :], al_ref[at, :]), gt, NN)
        for quad in range(d.cols // d.n):
            parts = [o_ref[p * d.g:(p + 1) * d.g, quad * LANES:(quad + 1) * LANES] for p in range(d.n)]
            for t, x in enumerate(swap_blocks(parts)):
                tb_ref[pl.ds(quad * d.n + t, d.g, stride=d.cols), :] = x
        for v in range(d.g):
            gb_ref[m, :, v * LANES:(v + 1) * LANES] = tb_ref[pl.ds(v * d.cols, d.cols), :]
    for m in range(d.R):
        at = slice(m * d.slab, (m + 1) * d.slab)
        out = dot3((xh_ref[at, :], xl_ref[at, :]), gt, NT) * (1.0 / d.S)
        for quad in range(d.rows // d.n):
            parts = [out[p * d.g:(p + 1) * d.g, quad * LANES:(quad + 1) * LANES] for p in range(d.n)]
            for t, x in enumerate(swap_blocks(parts)):
                ta_ref[pl.ds(quad * d.n + t, d.g, stride=d.rows), :] = x
        for k in range(d.per):
            dst = place(((r ^ m) * d.per + k) ^ q, order)
            for v in range(d.gb):
                ga_ref[dst, :, v * LANES:(v + 1) * LANES] = ta_ref[pl.ds((k * d.gb + v) * d.rows, d.rows), :]


def last_kernel(blocks, per, mine_ref, other_ref, w_ref, bias_ref):
    beta = blocks.mine()
    half = blocks.count // 2
    for t in range(half):
        at = pl.multiple_of((t ^ beta) * per, per)
        w_ref[pl.ds(at, per), :] = mine_ref[t, 0:per, :]
        at = pl.multiple_of(((t + half) ^ beta) * per, per)
        w_ref[pl.ds(at, per), :] = other_ref[t, 0:per, :]
    bias_ref[...] = mine_ref[0, per:per + 8, :]


def swap_with(x, axis, bit, size):
    return lax.ppermute(x, axis, [(i, i ^ (1 << bit)) for i in range(size)])


class Blocks:
    def __init__(self, bits):
        self.bits = bits
        self.count = 1 << len(bits)

    def mine(self):
        p = 0
        for axis, bit in self.bits:
            p = (p << 1) | ((lax.axis_index(axis) >> bit) & 1)
        return p


def call(kernel, outs, scratch, *args):
    return pl.pallas_call(
        kernel,
        out_shape=outs,
        scratch_shapes=[pltpu.VMEM(s, jnp.float32) for s in scratch],
        compiler_params=pltpu.CompilerParams(vmem_limit_bytes=48 << 20),
    )(*args)


def shape(*dims, dtype=jnp.float32):
    return jax.ShapeDtypeStruct(dims, dtype)


def build(mesh):
    size = {"row": mesh.shape["row"], "col": mesh.shape["col"]}
    count = {axis: n.bit_length() - 1 for axis, n in size.items()}
    order = list(range(2, count["col"])) + [b for b in (1, 0) if b < count["col"]]

    def local(side_a, side_b, pair_grad, out_weight):
        d = Dims(mesh, side_a, side_b, pair_grad, out_weight)
        half = jnp.bfloat16
        taken = [("col", 0), ("col", 1), ("row", 0)]
        rest = [(x, b) for x in ("col", "row") for b in range(count[x]) if (x, b) not in taken]
        blocks = Blocks(taken)
        pairs = d.rows * d.cols
        t_s, tb_s, ta_s = (d.G * pairs, LANES), (d.g * d.cols, LANES), (d.g * d.rows, LANES)
        o_s = (max(d.S, d.IC), d.JE)

        right = side_b[None]
        for bit in range(count["row"]):
            right = jnp.concatenate([right, swap_with(right, "row", bit, d.R)])
        left = side_a[None]
        for bit in order:
            left = jnp.concatenate([left, swap_with(left, "col", bit, d.Q)])

        big, small = shape(d.IC, d.JE, dtype=half), shape(d.slab, d.JE, dtype=half)
        gh, gl, bh, bl = call(
            lambda *refs: first_kernel(d, *refs), [big, big, small, small], [t_s, tb_s], pair_grad, out_weight, side_b
        )
        amat, bmat = shape(d.S, d.IC, dtype=half), shape(d.S, d.JE, dtype=half)
        per = d.CE // blocks.count
        part, ah, al, xh, xl = call(
            lambda *refs: second_kernel(d, order, blocks, *refs),
            [shape(blocks.count, per + 8, d.K), amat, amat, bmat, bmat],
            [t_s, tb_s, ta_s, o_s],
            pair_grad, left, right[1:], bh, bl,
        )
        gb, ga = call(
            lambda *refs: third_kernel(d, order, *refs),
            [shape(d.R, d.cols, d.slab * d.C), shape(d.Q, d.rows, d.blk)],
            [tb_s, ta_s, (d.slab, d.JE)],
            gh, gl, ah, al, xh, xl,
        )
        for axis, bit in taken:
            n = part.shape[0] // 2
            part = part[:n] + swap_with(part[n:], axis, bit, size[axis])
        for axis, bit in rest:
            part = part + swap_with(part, axis, bit, size[axis])
        for axis, bit in taken[:0:-1]:
            part = jnp.concatenate([part, swap_with(part, axis, bit, size[axis])])
        other = swap_with(part, *taken[0], size[taken[0][0]])
        weight, bias = call(
            lambda *refs: last_kernel(blocks, per, *refs), [shape(d.CE, d.K), shape(8, d.K)], [], part, other
        )
        for bit in range(count["row"] - 1, -1, -1):
            n = gb.shape[0] // 2
            gb = gb[:n] + swap_with(gb[n:], "row", bit, d.R)
        for bit in order[::-1]:
            n = ga.shape[0] // 2
            ga = ga[:n] + swap_with(ga[n:], "col", bit, d.Q)
        return ga[0], gb[0], weight, bias[0]

    return local


def solution(mesh):
    in_specs = (P("row", "col"), P("col", "row"), P("row", "col", None), P())
    out_specs = (P("row", "col"), P("col", "row"), P(), P())
    return jax.shard_map(build(mesh), mesh=mesh, in_specs=in_specs, out_specs=out_specs, check_vma=False)
```

```python
import math

import jax
import jax.numpy as jnp
from jax import lax
from jax.experimental import pallas as pl
from jax.experimental.pallas import tpu as pltpu
from jax.sharding import PartitionSpec as P


LANES = 128
NT = (((1,), (1,)), ((), ()))
NN = (((1,), (0,)), ((), ()))


def split(x):
    hi = x.astype(jnp.bfloat16)
    lo = (x - hi.astype(jnp.float32)).astype(jnp.bfloat16)
    return hi, lo


def dot3(a, b, dims):
    def one(u, v):
        return lax.dot_general(u, v, dims, preferred_element_type=jnp.float32)

    return one(a[0], b[0]) + (one(a[0], b[1]) + one(a[1], b[0]))


def swap_blocks(parts):
    n = len(parts)
    width = LANES // n
    block = lax.broadcasted_iota(jnp.int32, parts[0].shape, 1) // width
    step = 1
    while step < n:
        low = (block & step) == 0
        done = list(parts)
        for t in range(n):
            if t & step == 0:
                p, r = parts[t], parts[t + step]
                done[t] = jnp.where(low, p, pltpu.roll(r, step * width, 1))
                done[t + step] = jnp.where(low, pltpu.roll(p, LANES - step * width, 1), r)
        parts = done
        step *= 2
    return parts


def place(m, order):
    p = 0
    for k, bit in enumerate(order):
        p = p | (((m >> bit) & 1) << k)
    return p


class Dims:
    def __init__(self, mesh, side_a, pair_grad, out_weight):
        self.R, self.Q = mesh.shape["row"], mesh.shape["col"]
        self.rows, self.cols, self.K = pair_grad.shape
        self.CE = out_weight.shape[0]
        self.C = math.isqrt(self.CE)
        self.S = side_a.shape[1] * self.Q // self.C
        self.n = LANES // self.C
        self.G = self.C // self.n
        self.slab = self.S // self.R
        self.g = self.slab // self.n
        self.blk = side_a.shape[1]
        self.gb = self.blk // LANES
        self.per = self.Q // self.R
        self.IC = self.rows * self.C
        self.JE = self.cols * self.C


def fetch(src_ref, dst_ref, sem):
    copy = pltpu.make_async_copy(src_ref, dst_ref, sem)
    copy.start()
    return copy


def grad_outer_kernel(d, pg_ref, w_ref, gh_ref, gl_ref, ph_ref, pl_ref, bias_ref, t_ref, pv_ref, wv_ref, sems):
    w_copy = fetch(w_ref, wv_ref, sems.at[0])
    p_copy = fetch(pg_ref, pv_ref, sems.at[1])
    pairs = d.rows * d.cols
    p_copy.wait()
    flat = pv_ref[...].reshape(pairs, d.K)
    pg = split(flat)
    ph_ref[...], pl_ref[...] = split(flat.T)
    bias_ref[...] = jnp.broadcast_to(jnp.sum(flat, axis=0, keepdims=True), (8, d.K))
    w_copy.wait()
    two = 2 if d.G % 2 == 0 else 1
    for u in range(0, d.G, two):
        w = jnp.concatenate(
            [wv_ref[pl.ds((p4 * d.G + v) * d.C, d.C), :] for v in range(u, u + two) for p4 in range(d.n)], axis=0
        )
        out = dot3(pg, split(w), NT)
        for v in range(two):
            t_ref[pl.ds((u + v) * pairs, pairs), :] = out[:, v * LANES:(v + 1) * LANES]

    def body(i, carry):
        for quad in range(d.cols // d.n):
            parts = [t_ref[pl.ds(i * d.cols + quad * d.n + t, d.G, stride=pairs), :] for t in range(d.n)]
            hi, lo = split(jnp.concatenate(swap_blocks(parts), axis=0))
            at = pl.multiple_of(i * d.C, d.C)
            gh_ref[pl.ds(at, d.C), quad * LANES:(quad + 1) * LANES] = hi
            gl_ref[pl.ds(at, d.C), quad * LANES:(quad + 1) * LANES] = lo
        return carry

    lax.fori_loop(0, d.rows, body, 0)


def own_right_kernel(d, b_ref, bh_ref, bl_ref, tb_ref, sem):
    copies = [
        fetch(b_ref.at[:, pl.ds(v * LANES, LANES)], tb_ref.at[pl.ds(v * d.cols, d.cols)], sem) for v in range(d.g)
    ]
    for copy in copies:
        copy.wait()
    swap_to_seq(d, bh_ref, bl_ref, 0, tb_ref)


def to_seq(d, b_ref, bh_ref, bl_ref, at, tb_ref):
    for v in range(d.g):
        tb_ref[pl.ds(v * d.cols, d.cols), :] = b_ref[:, v * LANES:(v + 1) * LANES]
    swap_to_seq(d, bh_ref, bl_ref, at, tb_ref)


def swap_to_seq(d, bh_ref, bl_ref, at, tb_ref):
    for quad in range(d.cols // d.n):
        parts = [tb_ref[pl.ds(quad * d.n + t, d.g, stride=d.cols), :] for t in range(d.n)]
        hi, lo = split(jnp.concatenate(swap_blocks(parts), axis=0))
        bh_ref[at:at + d.slab, quad * LANES:(quad + 1) * LANES] = hi
        bl_ref[at:at + d.slab, quad * LANES:(quad + 1) * LANES] = lo


def weight_kernel(d, order, blocks, ph_ref, pl_ref, bias_ref, a_ref, bx_ref, bh_ref, bl_ref, w_ref, ah_ref, al_ref, xh_ref, xl_ref,
                  t_ref, tb_ref, ta_ref, o_ref):
    r, q = lax.axis_index("row"), lax.axis_index("col")
    pairs = d.rows * d.cols
    xh_ref[0:d.slab, :] = bh_ref[...]
    xl_ref[0:d.slab, :] = bl_ref[...]
    for m in range(1, d.R):
        to_seq(d, bx_ref.at[m - 1], xh_ref, xl_ref, m * d.slab, tb_ref)
    for m in range(d.R):
        for k in range(d.per):
            src = place(((r ^ m) * d.per + k) ^ q, order)
            for v in range(d.gb):
                ta_ref[pl.ds((k * d.gb + v) * d.rows, d.rows), :] = a_ref[src, :, v * LANES:(v + 1) * LANES]
        for quad in range(d.rows // d.n):
            parts = [ta_ref[pl.ds(quad * d.n + t, d.g, stride=d.rows), :] for t in range(d.n)]
            o_ref[m * d.slab:(m + 1) * d.slab, quad * LANES:(quad + 1) * LANES] = jnp.concatenate(
                swap_blocks(parts), axis=0) * (1.0 / d.S)
    a = o_ref[0:d.S, 0:d.IC]
    hi, lo = split(a)
    ah_ref[...] = hi
    al_ref[...] = lo
    o_ref[0:d.IC, :] = dot3(split(a.T), (xh_ref[...], xl_ref[...]), NN)

    def body(i, carry):
        for quad in range(d.cols // d.n):
            parts = [o_ref[pl.ds(pl.multiple_of(i * d.C + p4 * d.G, d.G), d.G), quad * LANES:(quad + 1) * LANES]
                     for p4 in range(d.n)]
            for t, x in enumerate(swap_blocks(parts)):
                t_ref[pl.ds(i * d.cols + quad * d.n + t, d.G, stride=pairs), :] = x
        return carry

    lax.fori_loop(0, d.rows, body, 0)
    turned = ph_ref[...], pl_ref[...]
    beta = blocks.mine()
    per = d.CE // blocks.count
    for u in range(d.G):
        part = dot3(turned, split(t_ref[pl.ds(u * pairs, pairs), :]), NN).T
        for p4 in range(d.n):
            row = (p4 * d.G + u) * d.C
            w_ref[(row // per) ^ beta, pl.ds(row % per, d.C), :] = part[p4 * d.C:(p4 + 1) * d.C]
    for t in range(blocks.count):
        w_ref[t, pl.ds(per, 8), :] = bias_ref[...]


def right_grad_kernel(d, gh_ref, gl_ref, ah_ref, al_ref, gb_ref, tb_ref, o_ref):
    gt = gh_ref[...], gl_ref[...]
    for m in range(d.R):
        at = slice(m * d.slab, (m + 1) * d.slab)
        o_ref[...] = dot3((ah_ref[at, :], al_ref[at, :]), gt, NN)
        for quad in range(d.cols // d.n):
            parts = [o_ref[p * d.g:(p + 1) * d.g, quad * LANES:(quad + 1) * LANES] for p in range(d.n)]
            for t, x in enumerate(swap_blocks(parts)):
                tb_ref[pl.ds(quad * d.n + t, d.g, stride=d.cols), :] = x
        for v in range(d.g):
            gb_ref[m, :, v * LANES:(v + 1) * LANES] = tb_ref[pl.ds(v * d.cols, d.cols), :]


def left_grad_kernel(d, order, gh_ref, gl_ref, xh_ref, xl_ref, ga_ref, ta_ref):
    r, q = lax.axis_index("row"), lax.axis_index("col")
    gt = gh_ref[...], gl_ref[...]
    for m in range(d.R):
        at = slice(m * d.slab, (m + 1) * d.slab)
        out = dot3((xh_ref[at, :], xl_ref[at, :]), gt, NT) * (1.0 / d.S)
        for quad in range(d.rows // d.n):
            parts = [out[p * d.g:(p + 1) * d.g, quad * LANES:(quad + 1) * LANES] for p in range(d.n)]
            for t, x in enumerate(swap_blocks(parts)):
                ta_ref[pl.ds(quad * d.n + t, d.g, stride=d.rows), :] = x
        for k in range(d.per):
            dst = place(((r ^ m) * d.per + k) ^ q, order)
            for v in range(d.gb):
                ga_ref[dst, :, v * LANES:(v + 1) * LANES] = ta_ref[pl.ds((k * d.gb + v) * d.rows, d.rows), :]


def last_kernel(blocks, per, mine_ref, other_ref, w_ref, bias_ref):
    beta = blocks.mine()
    half = blocks.count // 2
    for t in range(half):
        at = pl.multiple_of((t ^ beta) * per, per)
        w_ref[pl.ds(at, per), :] = mine_ref[t, 0:per, :]
        at = pl.multiple_of(((t + half) ^ beta) * per, per)
        w_ref[pl.ds(at, per), :] = other_ref[t, 0:per, :]
    bias_ref[...] = mine_ref[0, per, :]


def swap_with(x, axis, bit, size):
    return lax.ppermute(x, axis, [(i, i ^ (1 << bit)) for i in range(size)])


class Blocks:
    def __init__(self, bits):
        self.bits = bits
        self.count = 1 << len(bits)

    def mine(self):
        p = 0
        for axis, bit in self.bits:
            p = (p << 1) | ((lax.axis_index(axis) >> bit) & 1)
        return p


VMEM, HBM = pltpu.MemorySpace.VMEM, pltpu.MemorySpace.HBM


def call(kernel, outs, scratch, *args, space=VMEM):
    return pl.pallas_call(
        kernel,
        out_shape=outs,
        in_specs=[pl.BlockSpec(memory_space=space)] * len(args),
        scratch_shapes=[pltpu.VMEM(s, jnp.float32) if isinstance(s, tuple) else s for s in scratch],
        compiler_params=pltpu.CompilerParams(vmem_limit_bytes=48 << 20),
    )(*args)


def hbm(x):
    return pltpu.with_memory_space_constraint(x, HBM)


def shape(*dims, dtype=jnp.float32):
    return jax.ShapeDtypeStruct(dims, dtype)


def counts(mesh):
    return {axis: n.bit_length() - 1 for axis, n in mesh.shape.items()}


def build(mesh):
    size, count = mesh.shape, counts(mesh)
    order = list(range(2, count["col"])) + [b for b in (1, 0) if b < count["col"]]

    def swap(x, axis, bit):
        return swap_with(x, axis, bit, size[axis])

    def halve(x, axis, bit):
        n = x.shape[0] // 2
        send = x[n:]
        other = swap(send, axis, bit)
        return x[:n] + other

    def double(x, axis, bit):
        other = swap(x, axis, bit)
        return jnp.concatenate([x, other])

    def local(side_a, side_b, pair_grad, out_weight):
        d = Dims(mesh, side_a, pair_grad, out_weight)
        low = jnp.bfloat16
        taken, rest = plan(count)
        blocks = Blocks(taken)
        pairs = d.rows * d.cols
        t_s, tb_s, ta_s = (d.G * pairs, LANES), (d.g * d.cols, LANES), (d.g * d.rows, LANES)
        dma = pltpu.SemaphoreType.DMA

        left = side_a[None]
        for bit in order:
            left = double(left, "col", bit)
        right = side_b[None]
        for bit in range(count["row"]):
            right = double(right, "row", bit)

        big, small, turn = shape(d.IC, d.JE, dtype=low), shape(d.slab, d.JE, dtype=low), shape(d.K, pairs, dtype=low)
        gh, gl, ph, plo, bias = call(
            lambda *refs: grad_outer_kernel(d, *refs), [big, big, turn, turn, shape(8, d.K)],
            [t_s, (d.rows, d.cols, d.K), (d.CE, d.K), dma((2,))], hbm(pair_grad), hbm(out_weight), space=HBM,
        )
        bh, bl = call(lambda *refs: own_right_kernel(d, *refs), [small, small], [tb_s, dma(())], hbm(side_b), space=HBM)
        amat, bmat = shape(d.S, d.IC, dtype=low), shape(d.S, d.JE, dtype=low)
        per = d.CE // blocks.count
        part, ah, al, xh, xl = call(
            lambda *refs: weight_kernel(d, order, blocks, *refs),
            [shape(blocks.count, per + 8, d.K), amat, amat, bmat, bmat],
            [t_s, tb_s, ta_s, (max(d.S, d.IC), d.JE)],
            ph, plo, bias, left, right[1:], bh, bl,
        )
        gb = call(
            lambda *refs: right_grad_kernel(d, *refs), shape(d.R, d.cols, d.slab * d.C),
            [tb_s, (d.slab, d.JE)], gh, gl, ah, al,
        )
        ga = call(lambda *refs: left_grad_kernel(d, order, *refs), shape(d.Q, d.rows, d.blk), [ta_s], gh, gl, xh, xl)
        for axis, bit in taken:
            part = halve(part, axis, bit)
        for axis, bit in rest:
            other = swap(part, axis, bit)
            part = part + other
        for axis, bit in taken[:0:-1]:
            part = double(part, axis, bit)
        other = swap(part, *taken[0])
        weight, bias = call(
            lambda *refs: last_kernel(blocks, per, *refs), [shape(d.CE, d.K), shape(d.K)], [], part, other
        )
        for bit in reversed(range(count["row"])):
            gb = halve(gb, "row", bit)
        for bit in order[::-1]:
            ga = halve(ga, "col", bit)
        return ga[0], gb[0], weight, bias

    return local


def plan(count):
    taken = [("col", b) for b in range(min(3, count["col"]))]
    rest = [("col", b) for b in range(3, count["col"])] + [("row", b) for b in range(count["row"])]
    return taken, rest


def solution(mesh):
    in_specs = (P("row", "col"), P("col", "row"), P("row", "col", None), P())
    out_specs = (P("row", "col"), P("col", "row"), P(), P())
    return jax.shard_map(build(mesh), mesh=mesh, in_specs=in_specs, out_specs=out_specs, check_vma=False)
```

```python
import math

import jax
import jax.numpy as jnp
from jax import lax
from jax.experimental import pallas as pl
from jax.experimental.pallas import tpu as pltpu
from jax.sharding import PartitionSpec as P


LANES = 128
NT = (((1,), (1,)), ((), ()))
NN = (((1,), (0,)), ((), ()))


def split(x):
    hi = x.astype(jnp.bfloat16)
    lo = (x - hi.astype(jnp.float32)).astype(jnp.bfloat16)
    return hi, lo


def dot3(a, b, dims):
    def one(u, v):
        return lax.dot_general(u, v, dims, preferred_element_type=jnp.float32)

    return one(a[0], b[0]) + (one(a[0], b[1]) + one(a[1], b[0]))


def swap_blocks(parts):
    n = len(parts)
    width = LANES // n
    block = lax.broadcasted_iota(jnp.int32, parts[0].shape, 1) // width
    step = 1
    while step < n:
        low = (block & step) == 0
        done = list(parts)
        for t in range(n):
            if t & step == 0:
                p, r = parts[t], parts[t + step]
                done[t] = jnp.where(low, p, pltpu.roll(r, step * width, 1))
                done[t + step] = jnp.where(low, pltpu.roll(p, LANES - step * width, 1), r)
        parts = done
        step *= 2
    return parts


def place(m, order):
    p = 0
    for k, bit in enumerate(order):
        p = p | (((m >> bit) & 1) << k)
    return p


class Dims:
    def __init__(self, mesh, side_a, pair_grad, out_weight):
        self.R, self.Q = mesh.shape["row"], mesh.shape["col"]
        self.rows, self.cols, self.K = pair_grad.shape
        self.CE = out_weight.shape[0]
        self.C = math.isqrt(self.CE)
        self.S = side_a.shape[1] * self.Q // self.C
        self.n = LANES // self.C
        self.G = self.C // self.n
        self.slab = self.S // self.R
        self.g = self.slab // self.n
        self.blk = side_a.shape[1]
        self.gb = self.blk // LANES
        self.per = self.Q // self.R
        self.IC = self.rows * self.C
        self.JE = self.cols * self.C


def fetch(src_ref, dst_ref, sem):
    copy = pltpu.make_async_copy(src_ref, dst_ref, sem)
    copy.start()
    return copy


def pair_kernel(d, pg_ref, w_ref, t_ref, ph_ref, pl_ref, bias_ref, pv_ref, wv_ref, sems):
    w_copy = fetch(w_ref, wv_ref, sems.at[0])
    p_copy = fetch(pg_ref, pv_ref, sems.at[1])
    pairs = d.rows * d.cols
    p_copy.wait()
    flat = pv_ref[...].reshape(pairs, d.K)
    pg = split(flat)
    ph_ref[...], pl_ref[...] = split(flat.T)
    bias_ref[...] = jnp.broadcast_to(jnp.sum(flat, axis=0, keepdims=True), (8, d.K))
    w_copy.wait()
    two = 2 if d.G % 2 == 0 else 1
    for u in range(0, d.G, two):
        w = jnp.concatenate(
            [wv_ref[pl.ds((p4 * d.G + v) * d.C, d.C), :] for v in range(u, u + two) for p4 in range(d.n)], axis=0
        )
        out = dot3(pg, split(w), NT)
        for v in range(two):
            t_ref[pl.ds((u + v) * pairs, pairs), :] = out[:, v * LANES:(v + 1) * LANES]


def grad_outer_kernel(d, t_ref, gh_ref, gl_ref):
    pairs = d.rows * d.cols
    for i in range(d.rows):
        for quad in range(d.cols // d.n):
            parts = [t_ref[pl.ds(i * d.cols + quad * d.n + t, d.G, stride=pairs), :] for t in range(d.n)]
            hi, lo = split(jnp.concatenate(swap_blocks(parts), axis=0))
            gh_ref[i * d.C:(i + 1) * d.C, quad * LANES:(quad + 1) * LANES] = hi
            gl_ref[i * d.C:(i + 1) * d.C, quad * LANES:(quad + 1) * LANES] = lo


def own_right_kernel(d, b_ref, bh_ref, bl_ref, tb_ref, sem):
    copies = [
        fetch(b_ref.at[:, pl.ds(v * LANES, LANES)], tb_ref.at[pl.ds(v * d.cols, d.cols)], sem) for v in range(d.g)
    ]
    for copy in copies:
        copy.wait()
    swap_to_seq(d, bh_ref, bl_ref, 0, tb_ref)


def to_seq(d, b_ref, bh_ref, bl_ref, at, tb_ref):
    for v in range(d.g):
        tb_ref[pl.ds(v * d.cols, d.cols), :] = b_ref[:, v * LANES:(v + 1) * LANES]
    swap_to_seq(d, bh_ref, bl_ref, at, tb_ref)


def swap_to_seq(d, bh_ref, bl_ref, at, tb_ref):
    for quad in range(d.cols // d.n):
        parts = [tb_ref[pl.ds(quad * d.n + t, d.g, stride=d.cols), :] for t in range(d.n)]
        hi, lo = split(jnp.concatenate(swap_blocks(parts), axis=0))
        bh_ref[at:at + d.slab, quad * LANES:(quad + 1) * LANES] = hi
        bl_ref[at:at + d.slab, quad * LANES:(quad + 1) * LANES] = lo


def weight_kernel(d, order, blocks, ph_ref, pl_ref, bias_ref, a_ref, bx_ref, bh_ref, bl_ref, w_ref, ah_ref, al_ref, xh_ref, xl_ref,
                  t_ref, tb_ref, ta_ref, o_ref):
    r, q = lax.axis_index("row"), lax.axis_index("col")
    pairs = d.rows * d.cols
    xh_ref[0:d.slab, :] = bh_ref[...]
    xl_ref[0:d.slab, :] = bl_ref[...]
    for m in range(1, d.R):
        to_seq(d, bx_ref.at[m - 1], xh_ref, xl_ref, m * d.slab, tb_ref)
    for m in range(d.R):
        for k in range(d.per):
            src = place(((r ^ m) * d.per + k) ^ q, order)
            for v in range(d.gb):
                ta_ref[pl.ds((k * d.gb + v) * d.rows, d.rows), :] = a_ref[src, :, v * LANES:(v + 1) * LANES]
        for quad in range(d.rows // d.n):
            parts = [ta_ref[pl.ds(quad * d.n + t, d.g, stride=d.rows), :] for t in range(d.n)]
            o_ref[m * d.slab:(m + 1) * d.slab, quad * LANES:(quad + 1) * LANES] = jnp.concatenate(
                swap_blocks(parts), axis=0) * (1.0 / d.S)
    a = o_ref[0:d.S, 0:d.IC]
    hi, lo = split(a)
    ah_ref[...] = hi
    al_ref[...] = lo
    o_ref[0:d.IC, :] = dot3(split(a.T), (xh_ref[...], xl_ref[...]), NN)

    for i in range(d.rows):
        for quad in range(d.cols // d.n):
            parts = [o_ref[pl.ds(i * d.C + p4 * d.G, d.G), quad * LANES:(quad + 1) * LANES] for p4 in range(d.n)]
            for t, x in enumerate(swap_blocks(parts)):
                t_ref[pl.ds(i * d.cols + quad * d.n + t, d.G, stride=pairs), :] = x
    turned = ph_ref[...], pl_ref[...]
    keys = blocks.key(0), blocks.key(1)
    per = d.CE // blocks.count
    for u in range(d.G):
        part = dot3(turned, split(t_ref[pl.ds(u * pairs, pairs), :]), NN).T
        for p4 in range(d.n):
            row = (p4 * d.G + u) * d.C
            block = row // per
            w_ref[block ^ keys[2 * block // blocks.count], pl.ds(row % per, d.C), :] = part[p4 * d.C:(p4 + 1) * d.C]
    for t in range(blocks.count):
        w_ref[t, pl.ds(per, 8), :] = bias_ref[...]


def right_grad_kernel(d, gh_ref, gl_ref, ah_ref, al_ref, gb_ref, tb_ref, o_ref):
    gt = gh_ref[...], gl_ref[...]
    for m in range(d.R):
        at = slice(m * d.slab, (m + 1) * d.slab)
        o_ref[...] = dot3((ah_ref[at, :], al_ref[at, :]), gt, NN)
        for quad in range(d.cols // d.n):
            parts = [o_ref[p * d.g:(p + 1) * d.g, quad * LANES:(quad + 1) * LANES] for p in range(d.n)]
            for t, x in enumerate(swap_blocks(parts)):
                tb_ref[pl.ds(quad * d.n + t, d.g, stride=d.cols), :] = x
        for v in range(d.g):
            gb_ref[m, :, v * LANES:(v + 1) * LANES] = tb_ref[pl.ds(v * d.cols, d.cols), :]


def left_grad_kernel(d, order, gh_ref, gl_ref, xh_ref, xl_ref, ga_ref, ta_ref):
    r, q = lax.axis_index("row"), lax.axis_index("col")
    gt = gh_ref[...], gl_ref[...]
    for m in range(d.R):
        at = slice(m * d.slab, (m + 1) * d.slab)
        out = dot3((xh_ref[at, :], xl_ref[at, :]), gt, NT) * (1.0 / d.S)
        for quad in range(d.rows // d.n):
            parts = [out[p * d.g:(p + 1) * d.g, quad * LANES:(quad + 1) * LANES] for p in range(d.n)]
            for t, x in enumerate(swap_blocks(parts)):
                ta_ref[pl.ds(quad * d.n + t, d.g, stride=d.rows), :] = x
        for k in range(d.per):
            dst = place(((r ^ m) * d.per + k) ^ q, order)
            for v in range(d.gb):
                ga_ref[dst, :, v * LANES:(v + 1) * LANES] = ta_ref[pl.ds((k * d.gb + v) * d.rows, d.rows), :]


def last_kernel(blocks, per, mine_ref, other_ref, w_ref, bias_ref):
    half = blocks.count // 2
    odd = lax.axis_index("col") & 1
    for ref, top, key in ((mine_ref, 0, blocks.key(odd)), (other_ref, half, blocks.key(1 - odd))):
        for t in range(half):
            at = pl.multiple_of(((t + top) ^ key) * per, per)
            w_ref[pl.ds(at, per), :] = ref[t, 0:per, :]
    bias_ref[...] = mine_ref[0, per, :]


def swap_with(x, axis, bits, size):
    return lax.ppermute(x, axis, [(i, i ^ (1 << bits[i & 1])) for i in range(size)])


class Blocks:
    def __init__(self, steps):
        self.steps = steps
        self.count = 1 << len(steps)

    def key(self, odd):
        q, p = lax.axis_index("col"), 0
        for step in self.steps:
            bit = jnp.where(odd, step[1], step[0]) if not isinstance(odd, int) else step[odd]
            p = (p << 1) | ((q >> bit) & 1)
        return p


VMEM, HBM = pltpu.MemorySpace.VMEM, pltpu.MemorySpace.HBM


def call(kernel, outs, scratch, *args, space=VMEM):
    return pl.pallas_call(
        kernel,
        out_shape=outs,
        in_specs=[pl.BlockSpec(memory_space=space)] * len(args),
        scratch_shapes=[pltpu.VMEM(s, jnp.float32) if isinstance(s, tuple) else s for s in scratch],
        compiler_params=pltpu.CompilerParams(vmem_limit_bytes=48 << 20),
    )(*args)


def hbm(x):
    return pltpu.with_memory_space_constraint(x, HBM)


def shape(*dims, dtype=jnp.float32):
    return jax.ShapeDtypeStruct(dims, dtype)


def counts(mesh):
    return {axis: n.bit_length() - 1 for axis, n in mesh.shape.items()}


def build(mesh):
    size, count = mesh.shape, counts(mesh)
    order = list(range(2, count["col"])) + [b for b in (1, 0) if b < count["col"]]

    def swap(x, axis, bit):
        return swap_with(x, axis, bit if isinstance(bit, tuple) else (bit, bit), size[axis])

    def halve(x, axis, bit):
        n = x.shape[0] // 2
        send = x[n:]
        other = swap(send, axis, bit)
        return x[:n] + other

    def double(x, axis, bit):
        other = swap(x, axis, bit)
        return jnp.concatenate([x, other])

    def local(side_a, side_b, pair_grad, out_weight):
        d = Dims(mesh, side_a, pair_grad, out_weight)
        low = jnp.bfloat16
        taken, rest = plan(count)
        blocks = Blocks([bits for _, bits in taken])
        pairs = d.rows * d.cols
        t_s, tb_s, ta_s = (d.G * pairs, LANES), (d.g * d.cols, LANES), (d.g * d.rows, LANES)
        dma = pltpu.SemaphoreType.DMA

        left = side_a[None]
        for bit in order:
            left = double(left, "col", bit)
        right = side_b[None]
        for bit in range(count["row"]):
            right = double(right, "row", bit)

        big, small, turn = shape(d.IC, d.JE, dtype=low), shape(d.slab, d.JE, dtype=low), shape(d.K, pairs, dtype=low)
        outer, ph, plo, bias = call(
            lambda *refs: pair_kernel(d, *refs), [shape(*t_s), turn, turn, shape(8, d.K)],
            [(d.rows, d.cols, d.K), (d.CE, d.K), dma((2,))], hbm(pair_grad), hbm(out_weight), space=HBM,
        )
        gh, gl = call(lambda *refs: grad_outer_kernel(d, *refs), [big, big], [], outer)
        bh, bl = call(lambda *refs: own_right_kernel(d, *refs), [small, small], [tb_s, dma(())], hbm(side_b), space=HBM)
        amat, bmat = shape(d.S, d.IC, dtype=low), shape(d.S, d.JE, dtype=low)
        per = d.CE // blocks.count
        part, ah, al, xh, xl = call(
            lambda *refs: weight_kernel(d, order, blocks, *refs),
            [shape(blocks.count, per + 8, d.K), amat, amat, bmat, bmat],
            [t_s, tb_s, ta_s, (max(d.S, d.IC), d.JE)],
            ph, plo, bias, left, right[1:], bh, bl,
        )
        gb = call(
            lambda *refs: right_grad_kernel(d, *refs), shape(d.R, d.cols, d.slab * d.C),
            [tb_s, (d.slab, d.JE)], gh, gl, ah, al,
        )
        ga = call(lambda *refs: left_grad_kernel(d, order, *refs), shape(d.Q, d.rows, d.blk), [ta_s], gh, gl, xh, xl)
        for axis, bit in taken:
            part = halve(part, axis, bit)
        for axis, bit in rest:
            other = swap(part, axis, bit)
            part = part + other
        for axis, bit in taken[:0:-1]:
            part = double(part, axis, bit)
        other = swap(part, *taken[0])
        weight, bias = call(
            lambda *refs: last_kernel(blocks, per, *refs), [shape(d.CE, d.K), shape(d.K)], [], part, other
        )
        for bit in reversed(range(count["row"])):
            gb = halve(gb, "row", bit)
        for bit in order[::-1]:
            ga = halve(ga, "col", bit)
        return ga[0], gb[0], weight, bias

    return local


def plan(count):
    n = min(3, count["col"])
    taken = [("col", (0, 0))] + [("col", (b, n - b)) for b in range(1, n)]
    rest = [("col", b) for b in range(n, count["col"])] + [("row", b) for b in range(count["row"])]
    return taken, rest


def solution(mesh):
    in_specs = (P("row", "col"), P("col", "row"), P("row", "col", None), P())
    out_specs = (P("row", "col"), P("col", "row"), P(), P())
    return jax.shard_map(build(mesh), mesh=mesh, in_specs=in_specs, out_specs=out_specs, check_vma=False)
```

```python
import math

import jax
import jax.numpy as jnp
from jax import lax
from jax.experimental import pallas as pl
from jax.experimental.pallas import tpu as pltpu
from jax.sharding import PartitionSpec as P


LANES = 128
NT = (((1,), (1,)), ((), ()))
NN = (((1,), (0,)), ((), ()))


def split(x):
    hi = x.astype(jnp.bfloat16)
    lo = (x - hi.astype(jnp.float32)).astype(jnp.bfloat16)
    return hi, lo


def dot3(a, b, dims):
    def one(u, v):
        return lax.dot_general(u, v, dims, preferred_element_type=jnp.float32)

    return one(a[0], b[0]) + (one(a[0], b[1]) + one(a[1], b[0]))


def swap_blocks(parts):
    n = len(parts)
    width = LANES // n
    block = lax.broadcasted_iota(jnp.int32, parts[0].shape, 1) // width
    if n == 4:
        return swap_four(parts, width, block)
    step = 1
    while step < n:
        low = (block & step) == 0
        done = list(parts)
        for t in range(n):
            if t & step == 0:
                p, r = parts[t], parts[t + step]
                done[t] = jnp.where(low, p, pltpu.roll(r, step * width, 1))
                done[t + step] = jnp.where(low, pltpu.roll(p, LANES - step * width, 1), r)
        parts = done
        step *= 2
    return parts


def swap_four(parts, width, block):
    even, left, outer = (block & 1) == 0, block < 2, (block == 0) | (block == 3)
    pairs = []
    for p, r in (parts[:2], parts[2:]):
        turned = pltpu.roll(jnp.where(even, r, p), width, 1)
        pairs.append((jnp.where(even, p, turned), jnp.where(even, turned, r)))
    (a, u), (b, v) = pairs
    turned = pltpu.roll(jnp.where(left, b, a), 2 * width, 1)
    kept = jnp.where(left, u, v)
    other = pltpu.roll(jnp.where(left, v, u), 2 * width, 1)
    return [
        jnp.where(left, a, turned),
        jnp.where(outer, other, kept),
        jnp.where(left, turned, b),
        jnp.where(outer, kept, other),
    ]


def place(m, order):
    p = 0
    for k, bit in enumerate(order):
        p = p | (((m >> bit) & 1) << k)
    return p


def odd_tiles(n):
    return (-(-n // 8) | 1) * 8


class Dims:
    def __init__(self, mesh, side_a, pair_grad, out_weight):
        self.R, self.Q = mesh.shape["row"], mesh.shape["col"]
        self.rows, self.cols, self.K = pair_grad.shape
        self.CE = out_weight.shape[0]
        self.C = math.isqrt(self.CE)
        self.S = side_a.shape[1] * self.Q // self.C
        self.n = LANES // self.C
        self.G = self.C // self.n
        self.slab = self.S // self.R
        self.g = self.slab // self.n
        self.blk = side_a.shape[1]
        self.gb = self.blk // LANES
        self.per = self.Q // self.R
        self.pairs = self.rows * self.cols
        self.t_pitch, self.b_pitch, self.a_pitch = (odd_tiles(x) for x in (self.pairs, self.cols, self.rows))
        self.IC = self.rows * self.C
        self.JE = self.cols * self.C


def fetch(src_ref, dst_ref, sem):
    copy = pltpu.make_async_copy(src_ref, dst_ref, sem)
    copy.start()
    return copy


def pair_kernel(d, pg_ref, w_ref, t_ref, ph_ref, pl_ref, bias_ref, pv_ref, wv_ref, sems):
    w_copy = fetch(w_ref, wv_ref, sems.at[0])
    p_copy = fetch(pg_ref, pv_ref, sems.at[1])
    p_copy.wait()
    flat = pv_ref[...].reshape(d.pairs, d.K)
    pg = split(flat)
    ph_ref[...], pl_ref[...] = split(flat.T)
    bias_ref[...] = jnp.broadcast_to(jnp.sum(flat, axis=0, keepdims=True), (8, d.K))
    w_copy.wait()
    two = 2 if d.G % 2 == 0 else 1
    for u in range(0, d.G, two):
        w = jnp.concatenate(
            [wv_ref[pl.ds((p4 * d.G + v) * d.C, d.C), :] for v in range(u, u + two) for p4 in range(d.n)], axis=0
        )
        out = dot3(pg, split(w), NT)
        for v in range(two):
            t_ref[pl.ds(u + v, d.pairs, stride=d.G), :] = out[:, v * LANES:(v + 1) * LANES]


def grad_outer_kernel(d, t_ref, gh_ref, gl_ref):
    quads = range(d.cols // d.n)
    for i in range(d.rows):
        at = i * d.cols
        parts = [
            jnp.concatenate([t_ref[pl.ds((at + quad * d.n + t) * d.G, d.G), :] for quad in quads], axis=0)
            for t in range(d.n)
        ]
        done = swap_blocks(parts)
        for quad in quads:
            hi, lo = split(jnp.concatenate([x[quad * d.G:(quad + 1) * d.G] for x in done], axis=0))
            gh_ref[i * d.C:(i + 1) * d.C, quad * LANES:(quad + 1) * LANES] = hi
            gl_ref[i * d.C:(i + 1) * d.C, quad * LANES:(quad + 1) * LANES] = lo


def own_right_kernel(d, b_ref, bh_ref, bl_ref, tb_ref, sem):
    copies = [
        fetch(b_ref.at[:, pl.ds(v * LANES, LANES)], tb_ref.at[pl.ds(v * d.b_pitch, d.cols)], sem) for v in range(d.g)
    ]
    for copy in copies:
        copy.wait()
    swap_to_seq(d, bh_ref, bl_ref, 0, tb_ref)


def to_seq(d, b_ref, bh_ref, bl_ref, at, tb_ref):
    for v in range(d.g):
        tb_ref[pl.ds(v * d.b_pitch, d.cols), :] = b_ref[:, v * LANES:(v + 1) * LANES]
    swap_to_seq(d, bh_ref, bl_ref, at, tb_ref)


def swap_to_seq(d, bh_ref, bl_ref, at, tb_ref):
    for quad in range(d.cols // d.n):
        parts = [tb_ref[pl.ds(quad * d.n + t, d.g, stride=d.b_pitch), :] for t in range(d.n)]
        hi, lo = split(jnp.concatenate(swap_blocks(parts), axis=0))
        bh_ref[at:at + d.slab, quad * LANES:(quad + 1) * LANES] = hi
        bl_ref[at:at + d.slab, quad * LANES:(quad + 1) * LANES] = lo


def weight_kernel(d, order, blocks, ph_ref, pl_ref, bias_ref, a_ref, bx_ref, bh_ref, bl_ref, w_ref, ah_ref, al_ref, xh_ref, xl_ref,
                  t_ref, tb_ref, ta_ref, o_ref):
    r, q = lax.axis_index("row"), lax.axis_index("col")
    xh_ref[0:d.slab, :] = bh_ref[...]
    xl_ref[0:d.slab, :] = bl_ref[...]
    for m in range(1, d.R):
        to_seq(d, bx_ref.at[m - 1], xh_ref, xl_ref, m * d.slab, tb_ref)
    for m in range(d.R):
        for k in range(d.per):
            src = place(((r ^ m) * d.per + k) ^ q, order)
            for v in range(d.gb):
                ta_ref[pl.ds((k * d.gb + v) * d.a_pitch, d.rows), :] = a_ref[src, :, v * LANES:(v + 1) * LANES]
        for quad in range(d.rows // d.n):
            parts = [ta_ref[pl.ds(quad * d.n + t, d.g, stride=d.a_pitch), :] for t in range(d.n)]
            o_ref[m * d.slab:(m + 1) * d.slab, quad * LANES:(quad + 1) * LANES] = jnp.concatenate(
                swap_blocks(parts), axis=0) * (1.0 / d.S)
    a = o_ref[0:d.S, 0:d.IC]
    hi, lo = split(a)
    ah_ref[...] = hi
    al_ref[...] = lo
    o_ref[0:d.IC, :] = dot3(split(a.T), (xh_ref[...], xl_ref[...]), NN)

    quads = range(d.cols // d.n)
    for i in range(d.rows):
        parts = [
            jnp.concatenate(
                [o_ref[pl.ds(i * d.C + p4 * d.G, d.G), quad * LANES:(quad + 1) * LANES] for quad in quads], axis=0
            )
            for p4 in range(d.n)
        ]
        for t, x in enumerate(swap_blocks(parts)):
            for quad in quads:
                t_ref[pl.ds(i * d.cols + quad * d.n + t, d.G, stride=d.t_pitch), :] = x[quad * d.G:(quad + 1) * d.G]
    turned = ph_ref[...], pl_ref[...]
    keys = blocks.key(0), blocks.key(1)
    per = d.CE // blocks.count
    for u in range(d.G):
        part = dot3(turned, split(t_ref[pl.ds(u * d.t_pitch, d.pairs), :]), NN).T
        for p4 in range(d.n):
            row = (p4 * d.G + u) * d.C
            block = row // per
            w_ref[block ^ keys[2 * block // blocks.count], pl.ds(row % per, d.C), :] = part[p4 * d.C:(p4 + 1) * d.C]
    for t in range(blocks.count):
        w_ref[t, pl.ds(per, 8), :] = bias_ref[...]


def right_grad_kernel(d, gh_ref, gl_ref, ah_ref, al_ref, gb_ref, tb_ref, o_ref):
    gt = gh_ref[...], gl_ref[...]
    for m in range(d.R):
        at = slice(m * d.slab, (m + 1) * d.slab)
        o_ref[...] = dot3((ah_ref[at, :], al_ref[at, :]), gt, NN)
        for quad in range(d.cols // d.n):
            parts = [o_ref[p * d.g:(p + 1) * d.g, quad * LANES:(quad + 1) * LANES] for p in range(d.n)]
            for t, x in enumerate(swap_blocks(parts)):
                tb_ref[pl.ds(quad * d.n + t, d.g, stride=d.b_pitch), :] = x
        for v in range(d.g):
            gb_ref[m, :, v * LANES:(v + 1) * LANES] = tb_ref[pl.ds(v * d.b_pitch, d.cols), :]


def left_grad_kernel(d, order, gh_ref, gl_ref, xh_ref, xl_ref, ga_ref, ta_ref):
    r, q = lax.axis_index("row"), lax.axis_index("col")
    gt = gh_ref[...], gl_ref[...]
    for m in range(d.R):
        at = slice(m * d.slab, (m + 1) * d.slab)
        out = dot3((xh_ref[at, :], xl_ref[at, :]), gt, NT) * (1.0 / d.S)
        for quad in range(d.rows // d.n):
            parts = [out[p * d.g:(p + 1) * d.g, quad * LANES:(quad + 1) * LANES] for p in range(d.n)]
            for t, x in enumerate(swap_blocks(parts)):
                ta_ref[pl.ds(quad * d.n + t, d.g, stride=d.a_pitch), :] = x
        for k in range(d.per):
            dst = place(((r ^ m) * d.per + k) ^ q, order)
            for v in range(d.gb):
                ga_ref[dst, :, v * LANES:(v + 1) * LANES] = ta_ref[pl.ds((k * d.gb + v) * d.a_pitch, d.rows), :]


def last_kernel(blocks, per, mine_ref, other_ref, w_ref, bias_ref):
    half = blocks.count // 2
    odd = lax.axis_index("col") & 1
    for ref, top, key in ((mine_ref, 0, blocks.key(odd)), (other_ref, half, blocks.key(1 - odd))):
        for t in range(half):
            at = pl.multiple_of(((t + top) ^ key) * per, per)
            w_ref[pl.ds(at, per), :] = ref[t, 0:per, :]
    bias_ref[...] = mine_ref[0, per, :]


def swap_with(x, axis, bits, size):
    return lax.ppermute(x, axis, [(i, i ^ (1 << bits[i & 1])) for i in range(size)])


class Blocks:
    def __init__(self, steps):
        self.steps = steps
        self.count = 1 << len(steps)

    def key(self, odd):
        q, p = lax.axis_index("col"), 0
        for step in self.steps:
            bit = jnp.where(odd, step[1], step[0]) if not isinstance(odd, int) else step[odd]
            p = (p << 1) | ((q >> bit) & 1)
        return p


VMEM, HBM = pltpu.MemorySpace.VMEM, pltpu.MemorySpace.HBM


def call(kernel, outs, scratch, *args, space=VMEM):
    return pl.pallas_call(
        kernel,
        out_shape=outs,
        in_specs=[pl.BlockSpec(memory_space=space)] * len(args),
        scratch_shapes=[pltpu.VMEM(s, jnp.float32) if isinstance(s, tuple) else s for s in scratch],
        compiler_params=pltpu.CompilerParams(vmem_limit_bytes=48 << 20),
    )(*args)


def hbm(x):
    return pltpu.with_memory_space_constraint(x, HBM)


def shape(*dims, dtype=jnp.float32):
    return jax.ShapeDtypeStruct(dims, dtype)


def counts(mesh):
    return {axis: n.bit_length() - 1 for axis, n in mesh.shape.items()}


def build(mesh):
    size, count = mesh.shape, counts(mesh)
    order = list(range(2, count["col"])) + [b for b in (1, 0) if b < count["col"]]

    def swap(x, axis, bit):
        return swap_with(x, axis, bit if isinstance(bit, tuple) else (bit, bit), size[axis])

    def halve(x, axis, bit):
        n = x.shape[0] // 2
        send = x[n:]
        other = swap(send, axis, bit)
        return x[:n] + other

    def double(x, axis, bit):
        other = swap(x, axis, bit)
        return jnp.concatenate([x, other])

    def local(side_a, side_b, pair_grad, out_weight):
        d = Dims(mesh, side_a, pair_grad, out_weight)
        low = jnp.bfloat16
        taken, rest = plan(count)
        blocks = Blocks([bits for _, bits in taken])
        t_s, tb_s, ta_s = (d.G * d.t_pitch, LANES), (d.g * d.b_pitch, LANES), (d.g * d.a_pitch, LANES)
        dma = pltpu.SemaphoreType.DMA

        left = side_a[None]
        for bit in order:
            left = double(left, "col", bit)
        right = side_b[None]
        for bit in range(count["row"]):
            right = double(right, "row", bit)

        big, small, turn = shape(d.IC, d.JE, dtype=low), shape(d.slab, d.JE, dtype=low), shape(d.K, d.pairs, dtype=low)
        outer, ph, plo, bias = call(
            lambda *refs: pair_kernel(d, *refs), [shape(d.pairs * d.G, LANES), turn, turn, shape(8, d.K)],
            [(d.rows, d.cols, d.K), (d.CE, d.K), dma((2,))], hbm(pair_grad), hbm(out_weight), space=HBM,
        )
        gh, gl = call(lambda *refs: grad_outer_kernel(d, *refs), [big, big], [], outer)
        bh, bl = call(lambda *refs: own_right_kernel(d, *refs), [small, small], [tb_s, dma(())], hbm(side_b), space=HBM)
        amat, bmat = shape(d.S, d.IC, dtype=low), shape(d.S, d.JE, dtype=low)
        per = d.CE // blocks.count
        part, ah, al, xh, xl = call(
            lambda *refs: weight_kernel(d, order, blocks, *refs),
            [shape(blocks.count, per + 8, d.K), amat, amat, bmat, bmat],
            [t_s, tb_s, ta_s, (max(d.S, d.IC), d.JE)],
            ph, plo, bias, left, right[1:], bh, bl,
        )
        gb = call(
            lambda *refs: right_grad_kernel(d, *refs), shape(d.R, d.cols, d.slab * d.C),
            [tb_s, (d.slab, d.JE)], gh, gl, ah, al,
        )
        ga = call(lambda *refs: left_grad_kernel(d, order, *refs), shape(d.Q, d.rows, d.blk), [ta_s], gh, gl, xh, xl)
        for axis, bit in taken:
            part = halve(part, axis, bit)
        for axis, bit in rest:
            other = swap(part, axis, bit)
            part = part + other
        for axis, bit in taken[:0:-1]:
            part = double(part, axis, bit)
        other = swap(part, *taken[0])
        weight, bias = call(
            lambda *refs: last_kernel(blocks, per, *refs), [shape(d.CE, d.K), shape(d.K)], [], part, other
        )
        for bit in reversed(range(count["row"])):
            gb = halve(gb, "row", bit)
        for bit in order[::-1]:
            ga = halve(ga, "col", bit)
        return ga[0], gb[0], weight, bias

    return local


def plan(count):
    n = min(3, count["col"])
    taken = [("col", (0, 0))] + [("col", (b, b)) for b in range(1, n)]
    rest = [("col", b) for b in range(n, count["col"])] + [("row", b) for b in range(count["row"])]
    return taken, rest


def solution(mesh):
    in_specs = (P("row", "col"), P("col", "row"), P("row", "col", None), P())
    out_specs = (P("row", "col"), P("col", "row"), P(), P())
    return jax.shard_map(build(mesh), mesh=mesh, in_specs=in_specs, out_specs=out_specs, check_vma=False)
```
